256 devices in a mesh: tm: 32 (over x, z), space: 8 (over y, core).
Axes of the slice: x: 4, y: 4, z: 8, core: 2. Of those that a mesh axis runs over, the one named last changes fastest.
Arguments:
- queries: bfloat16 [32, 5120, 2240], P('tm', 'space'), may hold values from -6 to 6
- keys: bfloat16 [32, 5120, 2240], P('tm', 'space'), may hold values from -6 to 6
- values: bfloat16 [32, 5120, 2240], P('tm', 'space'), may hold values from -6 to 6
- gain: float32 [2240], replicated, may hold values from 0.1 to 1.9
- out_weight: bfloat16 [2240, 2240], P('tm'), may hold values from -0.125 to 0.125
Outputs:
- projected: bfloat16 [32, 5120, 2240], P('tm', 'space')
The draws below stay inside these ranges and needn't reach their ends.
All inputs are finite; a program needn't handle non-finite values.
Results may differ from the reference program's by a relative error of at most 0.0075.
Values may be sent and summed in bfloat16 or wider, within the bound.
No kernel may reach another device: no remote copies, remote signals or barrier semaphores. Data moves between devices by JAX's collectives and lax.ppermute only.
A program may use at most 128 MiB of HBM per device.

```python
import jax
import jax.numpy as jnp
from jax import lax

HEADS = 20
HEAD_DIM = 112
D = 2240
BLOCKS = 32
SPATIAL = 5120


def levels(stream_key, extent, split, smallest, largest):
    level = 1.0
    for axis_at, blocks in split:
        draws = jax.random.uniform(jax.random.fold_in(jax.random.fold_in(stream_key, 6), axis_at), (blocks,), jnp.float32, smallest / len(split), largest / len(split))
        level = level * jnp.repeat(jnp.exp(draws), extent[axis_at] // blocks).reshape((-1,) + (1,) * (len(extent) - 1 - axis_at))
    return level


def scatter_about(own_key, dims, deviation, limit, shards=(), kind=jnp.bfloat16):
    loudness = levels(own_key, dims, shards, -0.22, 0.18) if shards else 1.0
    entries = jax.random.normal(own_key, dims, jnp.float32) * deviation * loudness
    return jnp.minimum(jnp.maximum(entries, -limit), limit).astype(kind)


def setup_inputs(seed: int = 0) -> dict:
    seeds = jax.random.split(jax.random.key(seed), 6)
    return {
        "queries": scatter_about(seeds[0], (BLOCKS, SPATIAL, D), 1.0, 6.0, ((0, 32), (1, 8))),
        "keys": scatter_about(seeds[1], (BLOCKS, SPATIAL, D), 1.0, 6.0, ((0, 32), (1, 8))),
        "values": scatter_about(seeds[2], (BLOCKS, SPATIAL, D), 1.0, 6.0, ((0, 32), (1, 8))),
        "gain": jnp.clip(1.0 + 0.18 * jax.random.normal(seeds[3], (D,), jnp.float32), 0.1, 1.9),
        "out_weight": scatter_about(seeds[4], (D, D), D ** -0.5, 0.125, ((0, 32),)),
    }


def reference(queries, keys, values, gain, out_weight):

    def block_stats(pair):
        fk = jnp.maximum(pair[0], 0).astype(jnp.float32).reshape(SPATIAL, HEADS, HEAD_DIM)
        vals = pair[1].astype(jnp.float32).reshape(SPATIAL, HEADS, HEAD_DIM)
        state = jnp.einsum('shi,shj->hij', fk, vals, precision=lax.Precision.HIGHEST)
        return (state, lax.optimization_barrier(jnp.sum(fk, axis=0)))
    states, norms = lax.map(block_stats, (keys, values))
    states = jnp.cumsum(states, axis=0)
    norms = jnp.cumsum(norms, axis=0)

    def read_block(triple):
        fq = jnp.maximum(triple[0], 0).astype(jnp.float32).reshape(SPATIAL, HEADS, HEAD_DIM)
        numer = jnp.einsum('shi,hij->shj', fq, triple[1], precision=lax.Precision.HIGHEST)
        denom = jnp.einsum('shi,hi->sh', fq, triple[2], precision=lax.Precision.HIGHEST) + 1.0
        mixed = (numer / denom[:, :, None]).reshape(SPATIAL, D)
        meansq = lax.optimization_barrier(jnp.mean(mixed * mixed, axis=-1, keepdims=True))
        normed = (mixed * lax.rsqrt(meansq + 1e-06) * gain).astype(jnp.bfloat16)
        return jnp.dot(normed, out_weight, preferred_element_type=jnp.float32).astype(jnp.bfloat16)
    return lax.map(read_block, (queries, states, norms))
```

```python
import functools

import jax
import jax.numpy as jnp
from jax import lax
from jax.experimental import pallas as pl
from jax.experimental.pallas import tpu as pltpu
from jax.sharding import Mesh
from jax.sharding import PartitionSpec as P

HEADS = 20
HEAD_DIM = 112
D = HEADS * HEAD_DIM
PAD = 128
GROUP = 4
bf16 = jnp.bfloat16
f32 = jnp.float32
TM = ("x", "z")
PIECES = ("x", "y", "core")
NX, NZ, NY, NC = 4, 8, 4, 2
ROWS_X = D // NX
COLS = 2304
BIG = 40 * 1024 * 1024
SMALL = 12 * 1024 * 1024


def state_kernel(k_ref, v_ref, o_ref):
    tokens = k_ref.shape[1]
    ones = jnp.ones((PAD - HEAD_DIM, tokens), bf16)
    zeros = jnp.zeros((PAD - HEAD_DIM, tokens), bf16)
    for g in range(GROUP):
        rows = pl.ds(g * HEAD_DIM, HEAD_DIM)
        fk = jnp.concatenate([jnp.maximum(k_ref[rows, :], 0), zeros], axis=0)
        vals = jnp.concatenate([v_ref[rows, :], ones], axis=0)
        state = lax.dot_general(vals, fk, (((1,), (1,)), ((), ())), preferred_element_type=f32)
        o_ref[pl.ds(g * PAD, PAD), :] = state.astype(bf16)


def states(k_t, v_t):
    tokens = k_t.shape[1]
    spec = pl.BlockSpec((GROUP * HEAD_DIM, tokens), lambda i: (i, 0))
    return pl.pallas_call(
        state_kernel,
        grid=(HEADS // GROUP,),
        in_specs=[spec, spec],
        out_specs=pl.BlockSpec((GROUP * PAD, PAD), lambda i: (i, 0)),
        out_shape=jax.ShapeDtypeStruct((HEADS * PAD, PAD), bf16),
        compiler_params=pltpu.CompilerParams(vmem_limit_bytes=SMALL),
        name="states",
        cost_estimate=pl.CostEstimate(
            flops=2 * HEADS * PAD * PAD * tokens, bytes_accessed=4 * D * tokens, transcendentals=0
        ),
    )(k_t, v_t)


def in_tile_kernel(z_ref, r_ref, o_ref):
    z = z_ref[0]
    inclusive = None
    for x in range(NX):
        own = r_ref[x * 8].astype(f32)
        for s in range(1, 8):
            own = own + r_ref[x * 8 + s].astype(f32)
        exclusive = jnp.zeros_like(own) if inclusive is None else inclusive
        inclusive = exclusive + own
        later, earlier = inclusive.astype(bf16), exclusive.astype(bf16)
        for t in range(NZ):
            keep = (jnp.full(later.shape, t, jnp.int32) >= z).astype(f32)
            o_ref[t, x] = jnp.where(keep > 0, later.astype(f32), earlier.astype(f32)).astype(bf16)


def small_call(kernel, shape, name, scalars, arrays, scratch=()):
    return pl.pallas_call(
        kernel,
        in_specs=[pl.BlockSpec(memory_space=pltpu.SMEM)] * len(scalars)
        + [pl.BlockSpec(memory_space=pltpu.VMEM)] * len(arrays),
        out_specs=jax.tree.map(lambda _: pl.BlockSpec(memory_space=pltpu.VMEM), shape),
        out_shape=shape,
        scratch_shapes=list(scratch),
        compiler_params=pltpu.CompilerParams(vmem_limit_bytes=SMALL),
        name=name,
        cost_estimate=pl.CostEstimate(flops=1000000, bytes_accessed=2000000, transcendentals=0),
    )(*scalars, *arrays)


def prefix_kernel(r_ref, o_ref):
    for x in range(NX):
        total = r_ref[0, x].astype(f32)
        for t in range(1, NZ):
            total = total + r_ref[t, x].astype(f32)
        total = total.astype(bf16)
        for s in range(8):
            o_ref[x, s] = total


def slab_kernel(at_ref, w_ref, o_ref):
    slab, core = at_ref[0], at_ref[1]
    main = w_ref[:, pl.ds(pl.multiple_of(slab * 256, 256), 256)]
    first = w_ref[:, 2048:2176].astype(f32)
    last = w_ref[:, 2176:2240].astype(f32)
    last = jnp.concatenate([last, jnp.zeros_like(last)], axis=1)
    pick = (jnp.full(first.shape, core, jnp.int32) == 0)
    rest = jnp.where(pick, first, last).astype(bf16)
    for t in range(NZ):
        o_ref[t, :, :256] = main
        o_ref[t, :, 256:] = rest


def compact_kernel(w_ref, x_ref, y_ref, rows_ref):
    rows = w_ref.shape[1]
    for t in range(NZ):
        rows_ref[pl.ds(t * rows, rows), :] = w_ref[t].astype(f32)
    slab = rows_ref[...].astype(bf16)
    x_ref[:, :128] = slab[:, :128]
    x_ref[:, 128:] = slab[:, 256:]
    y_ref[...] = slab[:, 128:256]


def stack_kernel(*refs):
    by_x, by_y, (main_x, main_y, rest) = refs[:NX], refs[NX : NX + NY], refs[NX + NY :]
    for k in range(NX):
        main_x[k] = by_x[k][:, :128]
        rest[k] = by_x[k][:, 128:]
    for k in range(NY):
        main_y[k] = by_y[k][...]


def project_kernel(at_ref, q_ref, p_ref, g_ref, *refs):
    parts, (o_ref, w_ref, mixed_ref, normed_ref, sem) = refs[:18], refs[18:]
    x, y, core = at_ref[0], at_ref[1], at_ref[2]
    copies = []

    def fetch(source, block, column):
        rows = pl.ds(pl.multiple_of(block * ROWS_X, 16), ROWS_X)
        target = w_ref.at[rows, pl.ds(pl.multiple_of(column, 128), 128)]
        copies.append(pltpu.make_async_copy(source, target, sem.at[len(copies)]))
        copies[-1].start()

    for side in range(NC):
        which = core if side == 0 else 1 - core
        rest, by_y, by_x = parts[9 * side], parts[9 * side + 1 :][:4], parts[9 * side + 5 :][:4]
        for kx in range(NX):
            block = lax.rem(x - kx + NX, NX)
            fetch(rest.at[kx], block, 2048 + which * 128)
            for ky in range(NY):
                column = which * 1024 + lax.rem(y - ky + NY, NY) * 256
                fetch(by_y[ky].at[kx], block, column)
                fetch(by_x[kx].at[ky], block, column + 128)
    tokens = q_ref.shape[1]
    squares = jnp.zeros((1, tokens), f32)
    for h in range(HEADS):
        rows = pl.ds(h * HEAD_DIM, HEAD_DIM)
        fq = jnp.maximum(q_ref[rows, :], 0)
        prefix = p_ref[pl.ds(h * PAD, PAD), :][:, :HEAD_DIM]
        sums = jnp.dot(prefix, fq, preferred_element_type=f32)
        mixed = sums[:HEAD_DIM] * (1.0 / (sums[HEAD_DIM : HEAD_DIM + 1] + 1.0))
        squares = squares + jnp.sum(mixed * mixed, axis=0, keepdims=True)
        mixed_ref[rows, :] = mixed
    scale = lax.rsqrt(squares * (1.0 / D) + 1e-06)
    for i in range(0, D, 256):
        width = min(256, D - i)
        rows = pl.ds(i, width)
        normed = (mixed_ref[rows, :] * scale * g_ref[rows, :]).astype(bf16)
        normed_ref[:, pl.ds(i, width)] = normed.T
    for copy in copies:
        copy.wait()
    for j in range(0, D, 256):
        width = min(256, D - j)
        total = jnp.dot(normed_ref[...], w_ref[:, pl.ds(j, 256)], preferred_element_type=f32)
        o_ref[pl.ds(j, width), :] = total.astype(bf16).T[:width]


def project(at, q_t, prefix, gain, parts):
    tokens = q_t.shape[1]
    vmem = pl.BlockSpec(memory_space=pltpu.VMEM)
    anyw = pl.BlockSpec(memory_space=pl.ANY)
    return pl.pallas_call(
        project_kernel,
        in_specs=[pl.BlockSpec(memory_space=pltpu.SMEM), vmem, vmem, vmem] + [anyw] * 18,
        out_specs=vmem,
        out_shape=jax.ShapeDtypeStruct((D, tokens), bf16),
        scratch_shapes=[
            pltpu.VMEM((D, COLS), bf16),
            pltpu.VMEM((D, tokens), f32),
            pltpu.VMEM((tokens, D), bf16),
            pltpu.SemaphoreType.DMA((72,)),
        ],
        compiler_params=pltpu.CompilerParams(vmem_limit_bytes=BIG),
        name="project",
        cost_estimate=pl.CostEstimate(
            flops=2 * D * D * tokens, bytes_accessed=2 * D * COLS + 4 * D * tokens, transcendentals=0
        ),
    )(at, q_t, prefix, gain, *parts)


def swap(value, axes):
    return lax.all_to_all(value, axes, split_axis=0, concat_axis=0, tiled=True)


def shifted(value, axis):
    n = lax.axis_size(axis)
    return [
        lax.ppermute(value, axis, [(i, (i + k) % n) for i in range(n)]) for k in range(1, n)
    ]


def after(value, *others):
    return lax.optimization_barrier((value, *others))[0]


def local(queries, keys, values, gain, out_weight):
    tokens = queries.shape[1]
    q_t, k_t, v_t = (jnp.swapaxes(a[0], 0, 1) for a in (queries, keys, values))
    z, y, core = lax.axis_index("z"), lax.axis_index("y"), lax.axis_index("core")
    rows = out_weight.shape[0]
    at = jnp.stack([core * NY + y, core]).astype(jnp.int32)
    slabs = small_call(
        slab_kernel, jax.ShapeDtypeStruct((NZ, rows, 384), bf16), "slab", (at,), (out_weight,)
    )
    w_z = swap(slabs, "z")
    k_t, v_t = (pltpu.with_memory_space_constraint(a, pltpu.HBM) for a in (k_t, v_t))
    st = after(states(k_t, v_t), w_z)
    r1 = swap(st.reshape(32, 80, PAD), PIECES)
    w_x, w_y = small_call(
        compact_kernel,
        (jax.ShapeDtypeStruct((ROWS_X, 256), bf16), jax.ShapeDtypeStruct((ROWS_X, 128), bf16)),
        "compact",
        (),
        (w_z,),
        (pltpu.VMEM((NZ * rows, 384), f32),),
    )
    w_x = [w_x, *shifted(w_x, "x")]
    w_y = [w_y, *shifted(w_y, "y")]
    r2 = small_call(
        in_tile_kernel,
        jax.ShapeDtypeStruct((NZ, NX, 80, PAD), bf16),
        "in_tile",
        (z.astype(jnp.int32).reshape(1),),
        (r1,),
    )
    r2s = swap(r2, "z")
    four = jax.ShapeDtypeStruct((4, ROWS_X, 128), bf16)
    main_x, main_y, rest = small_call(
        stack_kernel, (four, four, four), "stack", (), [after(w, r2) for w in (*w_x, *w_y)]
    )
    parts = [rest, main_x, *shifted(main_x, "y"), main_y, *shifted(main_y, "x")]
    r3 = small_call(
        prefix_kernel, jax.ShapeDtypeStruct((NX, 8, 80, PAD), bf16), "prefix", (), (r2s,)
    )
    prefix = swap(r3.reshape(32, 80, PAD), PIECES).reshape(HEADS * PAD, PAD)
    parts += [lax.ppermute(part, "core", [(0, 1), (1, 0)]) for part in parts]
    at = jnp.stack([lax.axis_index("x"), y, core]).astype(jnp.int32)
    out = project(at, q_t, prefix, gain.reshape(D, 1), parts)
    return jnp.swapaxes(out, 0, 1)[None]


def solution(mesh):
    finer = Mesh(mesh.devices.reshape(NX, NZ, NY, NC), ("x", "z", "y", "core"))
    tokens = P(TM, ("y", "core"), None)
    return jax.shard_map(
        local,
        mesh=finer,
        in_specs=(tokens, tokens, tokens, P(), P(TM, None)),
        out_specs=tokens,
        check_vma=False,
    )
```

```python
import jax
import jax.numpy as jnp
from jax import lax
from jax.experimental import pallas as pl
from jax.experimental.pallas import tpu as pltpu
from jax.sharding import Mesh
from jax.sharding import PartitionSpec as P

HEADS = 20
HEAD_DIM = 112
D = HEADS * HEAD_DIM
PAD = 128
GROUP = 4
FULL = 18
PART = 64
bf16 = jnp.bfloat16
f32 = jnp.float32
TM = ("x", "z")
PIECES = ("x", "y", "core")
NX, NZ, NY, NC = 4, 8, 4, 2
ROWS_X = D // NX
COLS = 2304
BIG = 40 * 1024 * 1024
SMALL = 12 * 1024 * 1024


def state_kernel(k_ref, v_ref, o_ref, norm_ref):
    tokens = k_ref.shape[1]
    step = pl.program_id(0)
    ones = jnp.ones((PAD - HEAD_DIM, tokens), bf16)

    def state_of(g):
        rows = pl.ds(g * HEAD_DIM, HEAD_DIM)
        fk = jnp.maximum(k_ref[rows, :], 0)
        vals = jnp.concatenate([v_ref[rows, :], ones], axis=0)
        state = lax.dot_general(vals, fk, (((1,), (1,)), ((), ())), preferred_element_type=f32)
        state = jnp.concatenate([state, jnp.zeros((PAD, PAD - HEAD_DIM), f32)], axis=1)
        norm_ref[pl.ds(step * GROUP + g, 1), :] = state[HEAD_DIM : HEAD_DIM + 1]
        return state[:HEAD_DIM]

    @pl.when(step == 0)
    def _():
        norm_ref[...] = jnp.zeros_like(norm_ref)

    for g in range(2):
        at = pl.multiple_of((step * GROUP + g) * HEAD_DIM, 16)
        o_ref[pl.ds(at, HEAD_DIM), :] = state_of(g).astype(bf16)
    rest = [state_of(g) for g in range(2, GROUP)]

    @pl.when(step < HEADS // GROUP - 1)
    def _():
        for g in range(2, GROUP):
            at = pl.multiple_of((step * GROUP + g) * HEAD_DIM, 16)
            o_ref[pl.ds(at, HEAD_DIM), :] = rest[g - 2].astype(bf16)

    @pl.when(step == HEADS // GROUP - 1)
    def _():
        for g in range(2):
            for m in range(7):
                turned = pltpu.roll(rest[g], (HEAD_DIM - 16 * m) % PAD, 1).astype(bf16)
                o_ref[pl.ds((7 * g + m) * HEAD_DIM, HEAD_DIM), HEAD_DIM:] = turned[:, HEAD_DIM:]
        o_ref[pl.ds(FULL * HEAD_DIM, 32), :] = norm_ref[...].astype(bf16)


def states(k_t, v_t):
    tokens = k_t.shape[1]
    spec = pl.BlockSpec((GROUP * HEAD_DIM, tokens), lambda i: (i, 0))
    return pl.pallas_call(
        state_kernel,
        grid=(HEADS // GROUP,),
        in_specs=[spec, spec],
        out_specs=pl.BlockSpec((2048, PAD), lambda i: (0, 0)),
        out_shape=jax.ShapeDtypeStruct((2048, PAD), bf16),
        scratch_shapes=[pltpu.VMEM((32, PAD), f32)],
        compiler_params=pltpu.CompilerParams(vmem_limit_bytes=SMALL),
        name="states",
        cost_estimate=pl.CostEstimate(
            flops=2 * HEADS * PAD * PAD * tokens, bytes_accessed=4 * D * tokens, transcendentals=0
        ),
    )(k_t, v_t)


def in_tile_kernel(z_ref, r_ref, o_ref):
    z = z_ref[0]
    inclusive = None
    for x in range(NX):
        own = r_ref[x * 8].astype(f32)
        for s in range(1, 8):
            own = own + r_ref[x * 8 + s].astype(f32)
        exclusive = jnp.zeros_like(own) if inclusive is None else inclusive
        inclusive = exclusive + own
        later, earlier = inclusive.astype(bf16), exclusive.astype(bf16)
        for t in range(NZ):
            keep = (jnp.full(later.shape, t, jnp.int32) >= z).astype(f32)
            o_ref[t, x] = jnp.where(keep > 0, later.astype(f32), earlier.astype(f32)).astype(bf16)


def small_call(kernel, shape, scalars, arrays, scratch=()):
    return pl.pallas_call(
        kernel,
        in_specs=[pl.BlockSpec(memory_space=pltpu.SMEM)] * len(scalars)
        + [pl.BlockSpec(memory_space=pltpu.VMEM)] * len(arrays),
        out_specs=jax.tree.map(lambda _: pl.BlockSpec(memory_space=pltpu.VMEM), shape),
        out_shape=shape,
        scratch_shapes=list(scratch),
        compiler_params=pltpu.CompilerParams(vmem_limit_bytes=SMALL),
        cost_estimate=pl.CostEstimate(flops=1000000, bytes_accessed=2000000, transcendentals=0),
    )(*scalars, *arrays)


def prefix_kernel(r_ref, o_ref):
    for x in range(NX):
        total = r_ref[0, x].astype(f32)
        for t in range(1, NZ):
            total = total + r_ref[t, x].astype(f32)
        total = total.astype(bf16)
        for s in range(8):
            o_ref[x, s] = total


def slab_kernel(at_ref, w_ref, o_ref):
    slab, core = at_ref[0], at_ref[1]
    main = w_ref[:, pl.ds(pl.multiple_of(slab * 256, 256), 256)]
    first = w_ref[:, 2048:2176].astype(f32)
    last = w_ref[:, 2176:2240].astype(f32)
    last = jnp.concatenate([last, jnp.zeros_like(last)], axis=1)
    pick = jnp.full(first.shape, core, jnp.int32) == 0
    rest = jnp.where(pick, first, last).astype(bf16)
    for t in range(NZ):
        o_ref[t, :, :256] = main
        o_ref[t, :, 256:] = rest


def compact_kernel(w_ref, x_ref, y_ref, rows_ref):
    rows = w_ref.shape[1]
    for t in range(NZ):
        rows_ref[pl.ds(t * rows, rows), :] = w_ref[t].astype(f32)
    slab = rows_ref[...].astype(bf16)
    x_ref[0] = slab[:, :128]
    x_ref[1] = slab[:, 256:]
    y_ref[...] = slab[:, 128:256]


def stack_kernel(*refs):
    by_x, by_y, (main_x, main_y, every) = refs[:4], refs[4:8], refs[8:]
    for k in range(4):
        main_x[k] = by_x[k][0]
        main_y[k] = by_y[k][...]
        every[k] = by_x[k][1]
        every[4 + k] = by_x[k][0]
        every[8 + k] = by_y[k][...]


def project_kernel(at_ref, q_ref, p_ref, g_ref, *refs):
    parts, (o_ref, w_ref, mixed_ref, normed_ref, sem) = refs[:14], refs[14:]
    x, y, core = at_ref[0], at_ref[1], at_ref[2]
    groups = []

    def fetch(source, block, column):
        rows = pl.ds(pl.multiple_of(block * ROWS_X, 16), ROWS_X)
        at = sum(len(g) for g in groups)
        copy = pltpu.make_async_copy(source, w_ref.at[rows, pl.ds(column, 128)], sem.at[at])
        copy.start()
        groups[-1].append(copy)

    for side in range(NC):
        every, *rest = parts[7 * side : 7 * side + 7]
        by_y, by_x = (every.at[pl.ds(4, 4)], *rest[:3]), (every.at[pl.ds(8, 4)], *rest[3:])
        for n in range(4):
            groups.append([])
            for k in range(4):
                block = lax.rem(x - k + NX, NX)
                fetch(by_y[n].at[k], block, side * 1152 + n * 256)
                fetch(by_x[k].at[n], block, side * 1152 + n * 256 + 128)
        groups.append([])
        for k in range(4):
            fetch(every.at[k], lax.rem(x - k + NX, NX), side * 1152 + 1024)
    tokens = q_ref.shape[1]
    squares = jnp.zeros((1, tokens), f32)
    lane = lax.broadcasted_iota(jnp.int32, (HEAD_DIM, PAD), 1) // 16
    for h in range(HEADS):
        rows = pl.ds(h * HEAD_DIM, HEAD_DIM)
        fq = jnp.maximum(q_ref[rows, :], 0)
        if h < FULL:
            state = p_ref[rows, :]
        else:
            state = jnp.zeros((HEAD_DIM, PAD), f32)
            for m in range(7):
                piece = p_ref[pl.ds((7 * (h - FULL) + m) * HEAD_DIM, HEAD_DIM), :].astype(f32)
                state = jnp.where(lane == m, pltpu.roll(piece, (16 + 16 * m) % PAD, 1), state)
            state = state.astype(bf16)
        norms = p_ref[pl.ds(FULL * HEAD_DIM + h // 16 * 16, 16), :]
        prefix = jnp.concatenate([state, norms], axis=0)[:, :HEAD_DIM]
        sums = jnp.dot(prefix, fq, preferred_element_type=f32)
        norm = sums[HEAD_DIM + h % 16 : HEAD_DIM + h % 16 + 1]
        mixed = sums[:HEAD_DIM] * (1.0 / (norm + 1.0))
        squares = squares + jnp.sum(mixed * mixed, axis=0, keepdims=True)
        mixed_ref[rows, :] = mixed
    scale = lax.rsqrt(squares * (1.0 / D) + 1e-06)
    for i in range(0, D, 256):
        width = min(256, D - i)
        rows = pl.ds(i, width)
        normed = (mixed_ref[rows, :] * scale * g_ref[rows, :]).astype(bf16)
        normed_ref[:, pl.ds(i, width)] = normed.T

    def product(group, column, width):
        for copy in group:
            copy.wait()
        total = jnp.dot(normed_ref[...], w_ref[:, pl.ds(column, width)], preferred_element_type=f32)
        return total.astype(bf16).T

    for side in range(NC):
        which = core if side == 0 else 1 - core
        for n in range(4):
            at = pl.multiple_of(which * 1024 + lax.rem(y - n + NY, NY) * 256, 256)
            o_ref[pl.ds(at, 256), :] = product(groups[5 * side + n], side * 1152 + n * 256, 256)
        total = product(groups[5 * side + 4], side * 1152 + 1024, 128)

        @pl.when(which == 0)
        def _():
            o_ref[2048:2176, :] = total

        @pl.when(which == 1)
        def _():
            o_ref[2176:, :] = total[:64]


def project(at, q_t, prefix, gain, parts):
    tokens = q_t.shape[1]
    vmem = pl.BlockSpec(memory_space=pltpu.VMEM)
    anyw = pl.BlockSpec(memory_space=pl.ANY)
    return pl.pallas_call(
        project_kernel,
        in_specs=[pl.BlockSpec(memory_space=pltpu.SMEM), vmem, vmem, vmem] + [anyw] * 14,
        out_specs=vmem,
        out_shape=jax.ShapeDtypeStruct((D, tokens), bf16),
        scratch_shapes=[
            pltpu.VMEM((D, COLS), bf16),
            pltpu.VMEM((D, tokens), f32),
            pltpu.VMEM((tokens, D), bf16),
            pltpu.SemaphoreType.DMA((72,)),
        ],
        compiler_params=pltpu.CompilerParams(vmem_limit_bytes=BIG),
        name="project",
        cost_estimate=pl.CostEstimate(
            flops=2 * D * D * tokens, bytes_accessed=2 * D * COLS + 4 * D * tokens, transcendentals=0
        ),
    )(at, q_t, prefix, gain, *parts)


def swap(value, axes):
    return lax.all_to_all(value, axes, split_axis=0, concat_axis=0, tiled=True)


def moved(value, axis, step):
    n = lax.axis_size(axis)
    return lax.ppermute(value, axis, [(i, (i + step) % n) for i in range(n)])


def shifted(value, axis):
    return [moved(value, axis, k) for k in range(1, lax.axis_size(axis))]


def after(value, *others):
    return lax.optimization_barrier((value, *others))[0]


def step(queries, keys, values, gain, out_weight):
    q_t, k_t, v_t = (jnp.swapaxes(a[0], 0, 1) for a in (queries, keys, values))
    z, y, core = lax.axis_index("z"), lax.axis_index("y"), lax.axis_index("core")
    rows = out_weight.shape[0]
    at = jnp.stack([core * NY + y, core]).astype(jnp.int32)
    zs = z.astype(jnp.int32).reshape(1)
    rows = out_weight.shape[0]
    slab = small_call(slab_kernel, jax.ShapeDtypeStruct((NZ, rows, 384), bf16), (at,), (out_weight,))
    w_z = swap(slab, "z")
    k_t, v_t = (pltpu.with_memory_space_constraint(a, pltpu.HBM) for a in (k_t, v_t))
    st = after(states(k_t, v_t), w_z)
    r1 = swap(st.reshape(32, PART, PAD), PIECES)
    x0, y0 = small_call(
        compact_kernel,
        (jax.ShapeDtypeStruct((2, ROWS_X, 128), bf16), jax.ShapeDtypeStruct((ROWS_X, 128), bf16)),
        (),
        (w_z,),
        (pltpu.VMEM((NZ * rows, 384), f32),),
    )
    by_x = [x0, *shifted(x0, "x")]
    by_y = [y0, *shifted(y0, "y")]
    r2 = small_call(in_tile_kernel, jax.ShapeDtypeStruct((NZ, NX, PART, PAD), bf16), (zs,), (r1,))
    r2s = swap(r2, "z")
    four = jax.ShapeDtypeStruct((4, ROWS_X, 128), bf16)
    main_x, main_y, every = small_call(
        stack_kernel,
        (four, four, jax.ShapeDtypeStruct((12, ROWS_X, 128), bf16)),
        (),
        (*by_x, *by_y),
    )
    parts = [every, *shifted(main_x, "y"), *shifted(main_y, "x")]
    r3 = small_call(prefix_kernel, jax.ShapeDtypeStruct((NX, 8, PART, PAD), bf16), (), (r2s,))
    prefix = swap(r3.reshape(32, PART, PAD), PIECES).reshape(2048, PAD)
    parts += [moved(part, "core", 1) for part in parts]
    at = jnp.stack([lax.axis_index("x"), y, core]).astype(jnp.int32)
    out = project(at, q_t, prefix, gain.reshape(D, 1), parts)
    return jnp.swapaxes(out, 0, 1)[None]


def solution(mesh):
    finer = Mesh(mesh.devices.reshape(NX, NZ, NY, NC), ("x", "z", "y", "core"))
    tokens = P(TM, ("y", "core"), None)
    return jax.shard_map(
        step,
        mesh=finer,
        in_specs=(tokens, tokens, tokens, P(), P(TM, None)),
        out_specs=tokens,
        check_vma=False,
    )
```

```python
import jax
import jax.numpy as jnp
from jax import lax
from jax.experimental import pallas as pl
from jax.experimental.pallas import tpu as pltpu
from jax.sharding import Mesh
from jax.sharding import PartitionSpec as P

HEADS = 20
HEAD_DIM = 112
D = HEADS * HEAD_DIM
PAD = 128
GROUP = 4
FULL = 18
PART = 64
bf16 = jnp.bfloat16
f32 = jnp.float32
TM = ("x", "z")
PIECES = ("x", "y", "core")
NX, NZ, NY, NC = 4, 8, 4, 2
ROWS_X = D // NX
COLS = 2304
BIG = 40 * 1024 * 1024
SMALL = 12 * 1024 * 1024


def state_kernel(k_ref, v_ref, o_ref, norm_ref):
    tokens = k_ref.shape[1]
    step = pl.program_id(0)
    ones = jnp.ones((PAD - HEAD_DIM, tokens), bf16)

    def state_of(g):
        rows = pl.ds(g * HEAD_DIM, HEAD_DIM)
        fk = jnp.maximum(k_ref[rows, :], 0)
        vals = jnp.concatenate([v_ref[rows, :], ones], axis=0)
        state = lax.dot_general(vals, fk, (((1,), (1,)), ((), ())), preferred_element_type=f32)
        state = jnp.concatenate([state, jnp.zeros((PAD, PAD - HEAD_DIM), f32)], axis=1)
        norm_ref[pl.ds(step * GROUP + g, 1), :] = state[HEAD_DIM : HEAD_DIM + 1]
        return state[:HEAD_DIM]

    @pl.when(step == 0)
    def _():
        norm_ref[...] = jnp.zeros_like(norm_ref)

    for g in range(2):
        at = pl.multiple_of((step * GROUP + g) * HEAD_DIM, 16)
        o_ref[pl.ds(at, HEAD_DIM), :] = state_of(g).astype(bf16)
    rest = [state_of(g) for g in range(2, GROUP)]

    @pl.when(step < HEADS // GROUP - 1)
    def _():
        for g in range(2, GROUP):
            at = pl.multiple_of((step * GROUP + g) * HEAD_DIM, 16)
            o_ref[pl.ds(at, HEAD_DIM), :] = rest[g - 2].astype(bf16)

    @pl.when(step == HEADS // GROUP - 1)
    def _():
        for g in range(2):
            for m in range(7):
                turned = pltpu.roll(rest[g], (HEAD_DIM - 16 * m) % PAD, 1).astype(bf16)
                o_ref[pl.ds((7 * g + m) * HEAD_DIM, HEAD_DIM), HEAD_DIM:] = turned[:, HEAD_DIM:]
        o_ref[pl.ds(FULL * HEAD_DIM, 32), :] = norm_ref[...].astype(bf16)


def states(k_t, v_t):
    tokens = k_t.shape[1]
    spec = pl.BlockSpec((GROUP * HEAD_DIM, tokens), lambda i: (i, 0))
    return pl.pallas_call(
        state_kernel,
        grid=(HEADS // GROUP,),
        in_specs=[spec, spec],
        out_specs=pl.BlockSpec((2048, PAD), lambda i: (0, 0)),
        out_shape=jax.ShapeDtypeStruct((2048, PAD), bf16),
        scratch_shapes=[pltpu.VMEM((32, PAD), f32)],
        compiler_params=pltpu.CompilerParams(vmem_limit_bytes=SMALL),
        name="states",
        cost_estimate=pl.CostEstimate(
            flops=2 * HEADS * PAD * PAD * tokens, bytes_accessed=4 * D * tokens, transcendentals=0
        ),
    )(k_t, v_t)


def in_tile_kernel(z_ref, r_ref, o_ref):
    z = z_ref[0]
    inclusive = None
    for x in range(NX):
        own = r_ref[x * 8].astype(f32)
        for s in range(1, 8):
            own = own + r_ref[x * 8 + s].astype(f32)
        exclusive = jnp.zeros_like(own) if inclusive is None else inclusive
        inclusive = exclusive + own
        later, earlier = inclusive.astype(bf16), exclusive.astype(bf16)
        for t in range(NZ):
            keep = (jnp.full(later.shape, t, jnp.int32) >= z).astype(f32)
            o_ref[t, x] = jnp.where(keep > 0, later.astype(f32), earlier.astype(f32)).astype(bf16)


def small_call(kernel, shape, scalars, arrays, scratch=()):
    return pl.pallas_call(
        kernel,
        in_specs=[pl.BlockSpec(memory_space=pltpu.SMEM)] * len(scalars)
        + [pl.BlockSpec(memory_space=pltpu.VMEM)] * len(arrays),
        out_specs=jax.tree.map(lambda _: pl.BlockSpec(memory_space=pltpu.VMEM), shape),
        out_shape=shape,
        scratch_shapes=list(scratch),
        compiler_params=pltpu.CompilerParams(vmem_limit_bytes=SMALL),
        cost_estimate=pl.CostEstimate(flops=1000000, bytes_accessed=2000000, transcendentals=0),
    )(*scalars, *arrays)


def prefix_kernel(r_ref, o_ref):
    for x in range(NX):
        total = r_ref[0, x].astype(f32)
        for t in range(1, NZ):
            total = total + r_ref[t, x].astype(f32)
        total = total.astype(bf16)
        for s in range(8):
            o_ref[x, s] = total


def slab_kernel(at_ref, w_ref, o_ref):
    slab, core = at_ref[0], at_ref[1]
    main = w_ref[:, pl.ds(pl.multiple_of(slab * 256, 256), 256)]
    first = w_ref[:, 2048:2176].astype(f32)
    last = w_ref[:, 2176:2240].astype(f32)
    last = jnp.concatenate([last, jnp.zeros_like(last)], axis=1)
    pick = jnp.full(first.shape, core, jnp.int32) == 0
    rest = jnp.where(pick, first, last).astype(bf16)
    for t in range(NZ):
        o_ref[t, :, :256] = main
        o_ref[t, :, 256:] = rest


def compact_kernel(w_ref, x_ref, y_ref, rows_ref):
    rows = w_ref.shape[1]
    for t in range(NZ):
        rows_ref[pl.ds(t * rows, rows), :] = w_ref[t].astype(f32)
    slab = rows_ref[...].astype(bf16)
    x_ref[0] = slab[:, :128]
    x_ref[1] = slab[:, 256:]
    y_ref[...] = slab[:, 128:256]


def stack_kernel(*refs):
    by_x, by_y, (main_x, main_y, every) = refs[:4], refs[4:8], refs[8:]
    for k in range(4):
        main_x[k] = by_x[k][0]
        main_y[k] = by_y[k][...]
        every[k] = by_x[k][1]
        every[4 + k] = by_x[k][0]
        every[8 + k] = by_y[k][...]


def project_kernel(at_ref, q_ref, p_ref, g_ref, *refs):
    parts, (o_ref, w_ref, mixed_ref, normed_ref, sem) = refs[:14], refs[14:]
    x, y, core = at_ref[0], at_ref[1], at_ref[2]
    copies = []

    def fetch(source, block, column):
        rows = pl.ds(pl.multiple_of(block * ROWS_X, 16), ROWS_X)
        target = w_ref.at[rows, pl.ds(pl.multiple_of(column, 128), 128)]
        copies.append(pltpu.make_async_copy(source, target, sem.at[len(copies)]))
        copies[-1].start()

    for side in range(NC):
        which = core if side == 0 else 1 - core
        every, *rest = parts[7 * side : 7 * side + 7]
        by_y, by_x = (every.at[pl.ds(4, 4)], *rest[:3]), (every.at[pl.ds(8, 4)], *rest[3:])
        for k in range(4):
            block = lax.rem(x - k + NX, NX)
            column = which * 1024 + lax.rem(y - k + NY, NY) * 256
            fetch(every.at[k], block, 2048 + which * 128)
            for n in range(4):
                turn = lax.rem(y - n + NY, NY)
                fetch(by_y[n].at[k], block, which * 1024 + turn * 256)
                turn = lax.rem(x - n + NX, NX)
                fetch(by_x[n].at[k], turn, column + 128)
    tokens = q_ref.shape[1]
    squares = jnp.zeros((1, tokens), f32)
    lane = lax.broadcasted_iota(jnp.int32, (HEAD_DIM, PAD), 1) // 16
    for h in range(HEADS):
        rows = pl.ds(h * HEAD_DIM, HEAD_DIM)
        fq = jnp.maximum(q_ref[rows, :], 0)
        if h < FULL:
            state = p_ref[rows, :]
        else:
            state = jnp.zeros((HEAD_DIM, PAD), f32)
            for m in range(7):
                piece = p_ref[pl.ds((7 * (h - FULL) + m) * HEAD_DIM, HEAD_DIM), :].astype(f32)
                state = jnp.where(lane == m, pltpu.roll(piece, (16 + 16 * m) % PAD, 1), state)
            state = state.astype(bf16)
        norms = p_ref[pl.ds(FULL * HEAD_DIM + h // 16 * 16, 16), :]
        prefix = jnp.concatenate([state, norms], axis=0)[:, :HEAD_DIM]
        sums = jnp.dot(prefix, fq, preferred_element_type=f32)
        norm = sums[HEAD_DIM + h % 16 : HEAD_DIM + h % 16 + 1]
        mixed = sums[:HEAD_DIM] * (1.0 / (norm + 1.0))
        squares = squares + jnp.sum(mixed * mixed, axis=0, keepdims=True)
        mixed_ref[rows, :] = mixed
    scale = lax.rsqrt(squares * (1.0 / D) + 1e-06)
    for i in range(0, D, 256):
        width = min(256, D - i)
        rows = pl.ds(i, width)
        normed = (mixed_ref[rows, :] * scale * g_ref[rows, :]).astype(bf16)
        normed_ref[:, pl.ds(i, width)] = normed.T
    for copy in copies:
        copy.wait()
    for j in range(0, D, 256):
        width = min(256, D - j)
        total = jnp.dot(normed_ref[...], w_ref[:, pl.ds(j, 256)], preferred_element_type=f32)
        o_ref[pl.ds(j, width), :] = total.astype(bf16).T[:width]


def project(at, q_t, prefix, gain, parts):
    tokens = q_t.shape[1]
    vmem = pl.BlockSpec(memory_space=pltpu.VMEM)
    anyw = pl.BlockSpec(memory_space=pl.ANY)
    return pl.pallas_call(
        project_kernel,
        in_specs=[pl.BlockSpec(memory_space=pltpu.SMEM), vmem, vmem, vmem] + [anyw] * 14,
        out_specs=vmem,
        out_shape=jax.ShapeDtypeStruct((D, tokens), bf16),
        scratch_shapes=[
            pltpu.VMEM((D, COLS), bf16),
            pltpu.VMEM((D, tokens), f32),
            pltpu.VMEM((tokens, D), bf16),
            pltpu.SemaphoreType.DMA((72,)),
        ],
        compiler_params=pltpu.CompilerParams(vmem_limit_bytes=BIG),
        name="project",
        cost_estimate=pl.CostEstimate(
            flops=2 * D * D * tokens, bytes_accessed=2 * D * COLS + 4 * D * tokens, transcendentals=0
        ),
    )(at, q_t, prefix, gain, *parts)


def swap(value, axes):
    return lax.all_to_all(value, axes, split_axis=0, concat_axis=0, tiled=True)


def moved(value, axis, step):
    n = lax.axis_size(axis)
    return lax.ppermute(value, axis, [(i, (i + step) % n) for i in range(n)])


def shifted(value, axis):
    return [moved(value, axis, k) for k in range(1, lax.axis_size(axis))]


def after(value, *others):
    return lax.optimization_barrier((value, *others))[0]


def step(queries, keys, values, gain, out_weight):
    q_t, k_t, v_t = (jnp.swapaxes(a[0], 0, 1) for a in (queries, keys, values))
    z, y, core = lax.axis_index("z"), lax.axis_index("y"), lax.axis_index("core")
    rows = out_weight.shape[0]
    at = jnp.stack([core * NY + y, core]).astype(jnp.int32)
    zs = z.astype(jnp.int32).reshape(1)
    rows = out_weight.shape[0]
    slab = small_call(slab_kernel, jax.ShapeDtypeStruct((NZ, rows, 384), bf16), (at,), (out_weight,))
    w_z = swap(slab, "z")
    k_t, v_t = (pltpu.with_memory_space_constraint(a, pltpu.HBM) for a in (k_t, v_t))
    st = after(states(k_t, v_t), w_z)
    r1 = swap(st.reshape(32, PART, PAD), PIECES)
    x0, y0 = small_call(
        compact_kernel,
        (jax.ShapeDtypeStruct((2, ROWS_X, 128), bf16), jax.ShapeDtypeStruct((ROWS_X, 128), bf16)),
        (),
        (w_z,),
        (pltpu.VMEM((NZ * rows, 384), f32),),
    )
    by_x = [x0, *shifted(x0, "x")]
    by_y = [y0, *shifted(y0, "y")]
    r2 = small_call(in_tile_kernel, jax.ShapeDtypeStruct((NZ, NX, PART, PAD), bf16), (zs,), (r1,))
    r2s = swap(r2, "z")
    four = jax.ShapeDtypeStruct((4, ROWS_X, 128), bf16)
    main_x, main_y, every = small_call(
        stack_kernel,
        (four, four, jax.ShapeDtypeStruct((12, ROWS_X, 128), bf16)),
        (),
        (*by_x, *by_y),
    )
    parts = [every, *shifted(main_x, "y"), *shifted(main_y, "x")]
    r3 = small_call(prefix_kernel, jax.ShapeDtypeStruct((NX, 8, PART, PAD), bf16), (), (r2s,))
    prefix = swap(r3.reshape(32, PART, PAD), PIECES).reshape(2048, PAD)
    parts += [moved(part, "core", 1) for part in parts]
    at = jnp.stack([lax.axis_index("x"), y, core]).astype(jnp.int32)
    out = project(at, q_t, prefix, gain.reshape(D, 1), parts)
    return jnp.swapaxes(out, 0, 1)[None]


def solution(mesh):
    finer = Mesh(mesh.devices.reshape(NX, NZ, NY, NC), ("x", "z", "y", "core"))
    tokens = P(TM, ("y", "core"), None)
    return jax.shard_map(
        step,
        mesh=finer,
        in_specs=(tokens, tokens, tokens, P(), P(TM, None)),
        out_specs=tokens,
        check_vma=False,
    )
```

```python
import jax
import jax.numpy as jnp
from jax import lax
from jax.experimental import pallas as pl
from jax.experimental.pallas import tpu as pltpu
from jax.sharding import Mesh
from jax.sharding import PartitionSpec as P

HEADS = 20
HEAD_DIM = 112
D = HEADS * HEAD_DIM
PAD = 128
GROUP = 4
FULL = 18
PART = 64
bf16 = jnp.bfloat16
f32 = jnp.float32
TM = ("x", "z")
PIECES = ("x", "y", "core")
NX, NZ, NY, NC = 4, 8, 4, 2
ROWS_X = D // NX
COLS = 2304
BIG = 40 * 1024 * 1024
SMALL = 12 * 1024 * 1024


def state_kernel(k_ref, v_ref, o_ref, norm_ref):
    tokens = k_ref.shape[1]
    step = pl.program_id(0)
    ones = jnp.ones((PAD - HEAD_DIM, tokens), bf16)

    def state_of(g):
        rows = pl.ds(g * HEAD_DIM, HEAD_DIM)
        fk = jnp.maximum(k_ref[rows, :], 0)
        vals = jnp.concatenate([v_ref[rows, :], ones], axis=0)
        state = lax.dot_general(vals, fk, (((1,), (1,)), ((), ())), preferred_element_type=f32)
        state = jnp.concatenate([state, jnp.zeros((PAD, PAD - HEAD_DIM), f32)], axis=1)
        norm_ref[pl.ds(step * GROUP + g, 1), :] = state[HEAD_DIM : HEAD_DIM + 1]
        return state[:HEAD_DIM]

    @pl.when(step == 0)
    def _():
        norm_ref[...] = jnp.zeros_like(norm_ref)

    for g in range(2):
        at = pl.multiple_of((step * GROUP + g) * HEAD_DIM, 16)
        o_ref[pl.ds(at, HEAD_DIM), :] = state_of(g).astype(bf16)
    rest = [state_of(g) for g in range(2, GROUP)]

    @pl.when(step < HEADS // GROUP - 1)
    def _():
        for g in range(2, GROUP):
            at = pl.multiple_of((step * GROUP + g) * HEAD_DIM, 16)
            o_ref[pl.ds(at, HEAD_DIM), :] = rest[g - 2].astype(bf16)

    @pl.when(step == HEADS // GROUP - 1)
    def _():
        for g in range(2):
            for m in range(7):
                turned = pltpu.roll(rest[g], (HEAD_DIM - 16 * m) % PAD, 1).astype(bf16)
                o_ref[pl.ds((7 * g + m) * HEAD_DIM, HEAD_DIM), HEAD_DIM:] = turned[:, HEAD_DIM:]
        o_ref[pl.ds(FULL * HEAD_DIM, 32), :] = norm_ref[...].astype(bf16)


def states(k_t, v_t):
    tokens = k_t.shape[1]
    spec = pl.BlockSpec((GROUP * HEAD_DIM, tokens), lambda i: (i, 0))
    return pl.pallas_call(
        state_kernel,
        grid=(HEADS // GROUP,),
        in_specs=[spec, spec],
        out_specs=pl.BlockSpec((2048, PAD), lambda i: (0, 0)),
        out_shape=jax.ShapeDtypeStruct((2048, PAD), bf16),
        scratch_shapes=[pltpu.VMEM((32, PAD), f32)],
        compiler_params=pltpu.CompilerParams(vmem_limit_bytes=SMALL),
        name="states",
        cost_estimate=pl.CostEstimate(
            flops=2 * HEADS * PAD * PAD * tokens, bytes_accessed=4 * D * tokens, transcendentals=0
        ),
    )(k_t, v_t)


def in_tile_kernel(z_ref, r_ref, o_ref):
    z = z_ref[0]
    inclusive = None
    for x in range(NX):
        own = r_ref[x * 8].astype(f32)
        for s in range(1, 8):
            own = own + r_ref[x * 8 + s].astype(f32)
        exclusive = jnp.zeros_like(own) if inclusive is None else inclusive
        inclusive = exclusive + own
        later, earlier = inclusive.astype(bf16), exclusive.astype(bf16)
        for t in range(NZ):
            keep = (jnp.full(later.shape, t, jnp.int32) >= z).astype(f32)
            o_ref[t, x] = jnp.where(keep > 0, later.astype(f32), earlier.astype(f32)).astype(bf16)


def small_call(kernel, shape, scalars, arrays, scratch=()):
    return pl.pallas_call(
        kernel,
        in_specs=[pl.BlockSpec(memory_space=pltpu.SMEM)] * len(scalars)
        + [pl.BlockSpec(memory_space=pltpu.VMEM)] * len(arrays),
        out_specs=jax.tree.map(lambda _: pl.BlockSpec(memory_space=pltpu.VMEM), shape),
        out_shape=shape,
        scratch_shapes=list(scratch),
        compiler_params=pltpu.CompilerParams(vmem_limit_bytes=SMALL),
        cost_estimate=pl.CostEstimate(flops=1000000, bytes_accessed=2000000, transcendentals=0),
    )(*scalars, *arrays)


def prefix_kernel(r_ref, o_ref):
    for x in range(NX):
        total = r_ref[0, x].astype(f32)
        for t in range(1, NZ):
            total = total + r_ref[t, x].astype(f32)
        total = total.astype(bf16)
        for s in range(8):
            o_ref[x, s] = total


def slab_kernel(at_ref, w_ref, o_ref):
    slab, core = at_ref[0], at_ref[1]
    main = w_ref[:, pl.ds(pl.multiple_of(slab * 256, 256), 256)]
    first = w_ref[:, 2048:2176].astype(f32)
    last = w_ref[:, 2176:2240].astype(f32)
    last = jnp.concatenate([last, jnp.zeros_like(last)], axis=1)
    pick = jnp.full(first.shape, core, jnp.int32) == 0
    rest = jnp.where(pick, first, last).astype(bf16)
    for t in range(NZ):
        o_ref[t, :, :256] = main
        o_ref[t, :, 256:] = rest


def compact_kernel(w_ref, x_ref, y_ref, r_ref, rows_ref):
    rows = w_ref.shape[1]
    for t in range(NZ):
        rows_ref[pl.ds(t * rows, rows), :] = w_ref[t].astype(f32)
    slab = rows_ref[...].astype(bf16)
    x_ref[...] = slab[:, :128]
    y_ref[...] = slab[:, 128:256]
    r_ref[...] = slab[:, 256:]


def stack_kernel(*refs):
    by_x, by_y, rest, (main_x, main_y, every) = refs[:4], refs[4:8], refs[8], refs[9:]
    for k in range(4):
        main_x[k] = by_x[k][...]
        main_y[k] = by_y[k][...]
        every[k] = by_x[k][...]
        every[4 + k] = by_y[k][...]
    every[8] = rest[...]


def project_kernel(at_ref, q_ref, p_ref, g_ref, *refs):
    parts, (o_ref, w_ref, mixed_ref, normed_ref, sem) = refs[:20], refs[20:]
    x, y, core = at_ref[0], at_ref[1], at_ref[2]
    copies = []

    def fetch(source, block, column):
        rows = pl.ds(pl.multiple_of(block * ROWS_X, 16), ROWS_X)
        target = w_ref.at[rows, pl.ds(pl.multiple_of(column, 128), 128)]
        copies.append(pltpu.make_async_copy(source, target, sem.at[len(copies)]))
        copies[-1].start()

    for side in range(NC):
        which = core if side == 0 else 1 - core
        every, *rest = parts[10 * side : 10 * side + 10]
        by_y, by_x = (every.at[pl.ds(0, 4)], *rest[:3]), (every.at[pl.ds(4, 4)], *rest[3:6])
        edges = (every.at[8], *rest[6:])
        for k in range(4):
            block = lax.rem(x - k + NX, NX)
            column = which * 1024 + lax.rem(y - k + NY, NY) * 256
            fetch(edges[k], block, 2048 + which * 128)
            for n in range(4):
                turn = lax.rem(y - n + NY, NY)
                fetch(by_y[n].at[k], block, which * 1024 + turn * 256)
                turn = lax.rem(x - n + NX, NX)
                fetch(by_x[n].at[k], turn, column + 128)
    tokens = q_ref.shape[1]
    squares = jnp.zeros((1, tokens), f32)
    lane = lax.broadcasted_iota(jnp.int32, (HEAD_DIM, PAD), 1) // 16
    for h in range(HEADS):
        rows = pl.ds(h * HEAD_DIM, HEAD_DIM)
        fq = jnp.maximum(q_ref[rows, :], 0)
        if h < FULL:
            state = p_ref[rows, :]
        else:
            state = jnp.zeros((HEAD_DIM, PAD), f32)
            for m in range(7):
                piece = p_ref[pl.ds((7 * (h - FULL) + m) * HEAD_DIM, HEAD_DIM), :].astype(f32)
                state = jnp.where(lane == m, pltpu.roll(piece, (16 + 16 * m) % PAD, 1), state)
            state = state.astype(bf16)
        norms = p_ref[pl.ds(FULL * HEAD_DIM + h // 16 * 16, 16), :]
        prefix = jnp.concatenate([state, norms], axis=0)[:, :HEAD_DIM]
        sums = jnp.dot(prefix, fq, preferred_element_type=f32)
        norm = sums[HEAD_DIM + h % 16 : HEAD_DIM + h % 16 + 1]
        mixed = sums[:HEAD_DIM] * (1.0 / (norm + 1.0))
        squares = squares + jnp.sum(mixed * mixed, axis=0, keepdims=True)
        mixed_ref[rows, :] = mixed
    scale = lax.rsqrt(squares * (1.0 / D) + 1e-06)
    for i in range(0, D, 256):
        width = min(256, D - i)
        rows = pl.ds(i, width)
        normed = (mixed_ref[rows, :] * scale * g_ref[rows, :]).astype(bf16)
        normed_ref[:, pl.ds(i, width)] = normed.T
    for copy in copies:
        copy.wait()
    for j in range(0, D, 256):
        width = min(256, D - j)
        total = jnp.dot(normed_ref[...], w_ref[:, pl.ds(j, 256)], preferred_element_type=f32)
        o_ref[pl.ds(j, width), :] = total.astype(bf16).T[:width]


def project(at, q_t, prefix, gain, parts):
    tokens = q_t.shape[1]
    vmem = pl.BlockSpec(memory_space=pltpu.VMEM)
    anyw = pl.BlockSpec(memory_space=pl.ANY)
    return pl.pallas_call(
        project_kernel,
        in_specs=[pl.BlockSpec(memory_space=pltpu.SMEM), vmem, vmem, vmem] + [anyw] * 20,
        out_specs=vmem,
        out_shape=jax.ShapeDtypeStruct((D, tokens), bf16),
        scratch_shapes=[
            pltpu.VMEM((D, COLS), bf16),
            pltpu.VMEM((D, tokens), f32),
            pltpu.VMEM((tokens, D), bf16),
            pltpu.SemaphoreType.DMA((72,)),
        ],
        compiler_params=pltpu.CompilerParams(vmem_limit_bytes=BIG),
        name="project",
        cost_estimate=pl.CostEstimate(
            flops=2 * D * D * tokens, bytes_accessed=2 * D * COLS + 4 * D * tokens, transcendentals=0
        ),
    )(at, q_t, prefix, gain, *parts)


def swap(value, axes):
    return lax.all_to_all(value, axes, split_axis=0, concat_axis=0, tiled=True)


def moved(value, axis, step):
    n = lax.axis_size(axis)
    return lax.ppermute(value, axis, [(i, (i + step) % n) for i in range(n)])


def shifted(value, axis):
    return [moved(value, axis, k) for k in range(1, lax.axis_size(axis))]


def after(value, *others):
    return lax.optimization_barrier((value, *others))[0]


def step(queries, keys, values, gain, out_weight):
    q_t, k_t, v_t = (jnp.swapaxes(a[0], 0, 1) for a in (queries, keys, values))
    z, y, core = lax.axis_index("z"), lax.axis_index("y"), lax.axis_index("core")
    rows = out_weight.shape[0]
    at = jnp.stack([core * NY + y, core]).astype(jnp.int32)
    zs = z.astype(jnp.int32).reshape(1)
    rows = out_weight.shape[0]
    slab = small_call(slab_kernel, jax.ShapeDtypeStruct((NZ, rows, 384), bf16), (at,), (out_weight,))
    w_z = swap(slab, "z")
    k_t, v_t = (pltpu.with_memory_space_constraint(a, pltpu.HBM) for a in (k_t, v_t))
    st = after(states(k_t, v_t), w_z)
    r1 = swap(st.reshape(32, PART, PAD), PIECES)
    x0, y0, r0 = small_call(
        compact_kernel,
        (jax.ShapeDtypeStruct((ROWS_X, 128), bf16),) * 3,
        (),
        (w_z,),
        (pltpu.VMEM((NZ * rows, 384), f32),),
    )
    by_x = [x0, *shifted(x0, "x")]
    by_y = [y0, *shifted(y0, "y")]
    r2 = small_call(in_tile_kernel, jax.ShapeDtypeStruct((NZ, NX, PART, PAD), bf16), (zs,), (r1,))
    r2s = swap(r2, "z")
    four = jax.ShapeDtypeStruct((4, ROWS_X, 128), bf16)
    main_x, main_y, every = small_call(
        stack_kernel,
        (four, four, jax.ShapeDtypeStruct((9, ROWS_X, 128), bf16)),
        (),
        (*by_x, *by_y, r0),
    )
    parts = [every, *shifted(main_x, "y"), *shifted(main_y, "x"), *shifted(r0, "x")]
    r3 = small_call(prefix_kernel, jax.ShapeDtypeStruct((NX, 8, PART, PAD), bf16), (), (r2s,))
    prefix = swap(r3.reshape(32, PART, PAD), PIECES).reshape(2048, PAD)
    parts += [moved(part, "core", 1) for part in parts]
    at = jnp.stack([lax.axis_index("x"), y, core]).astype(jnp.int32)
    out = project(at, q_t, prefix, gain.reshape(D, 1), parts)
    return jnp.swapaxes(out, 0, 1)[None]


def solution(mesh):
    finer = Mesh(mesh.devices.reshape(NX, NZ, NY, NC), ("x", "z", "y", "core"))
    tokens = P(TM, ("y", "core"), None)
    return jax.shard_map(
        step,
        mesh=finer,
        in_specs=(tokens, tokens, tokens, P(), P(TM, None)),
        out_specs=tokens,
        check_vma=False,
    )
```

```python
import jax
import jax.numpy as jnp
from jax import lax
from jax.experimental import pallas as pl
from jax.experimental.pallas import tpu as pltpu
from jax.sharding import Mesh
from jax.sharding import PartitionSpec as P

HEADS = 20
HEAD_DIM = 112
D = HEADS * HEAD_DIM
PAD = 128
GROUP = 4
FULL = 18
PART = 64
bf16 = jnp.bfloat16
f32 = jnp.float32
TM = ("x", "z")
PIECES = ("x", "y", "core")
NX, NZ, NY, NC = 4, 8, 4, 2
ROWS_X = D // NX
COLS = 2304
BIG = 40 * 1024 * 1024
SMALL = 12 * 1024 * 1024


def state_kernel(k_ref, v_ref, o_ref, norm_ref):
    tokens = k_ref.shape[1]
    step = pl.program_id(0)
    ones = jnp.ones((PAD - HEAD_DIM, tokens), bf16)

    def state_of(g):
        rows = pl.ds(g * HEAD_DIM, HEAD_DIM)
        fk = jnp.maximum(k_ref[rows, :], 0)
        vals = jnp.concatenate([v_ref[rows, :], ones], axis=0)
        state = lax.dot_general(vals, fk, (((1,), (1,)), ((), ())), preferred_element_type=f32)
        state = jnp.concatenate([state, jnp.zeros((PAD, PAD - HEAD_DIM), f32)], axis=1)
        norm_ref[pl.ds(step * GROUP + g, 1), :] = state[HEAD_DIM : HEAD_DIM + 1]
        return state[:HEAD_DIM]

    @pl.when(step == 0)
    def _():
        norm_ref[...] = jnp.zeros_like(norm_ref)

    for g in range(2):
        at = pl.multiple_of((step * GROUP + g) * HEAD_DIM, 16)
        o_ref[pl.ds(at, HEAD_DIM), :] = state_of(g).astype(bf16)
    rest = [state_of(g) for g in range(2, GROUP)]

    @pl.when(step < HEADS // GROUP - 1)
    def _():
        for g in range(2, GROUP):
            at = pl.multiple_of((step * GROUP + g) * HEAD_DIM, 16)
            o_ref[pl.ds(at, HEAD_DIM), :] = rest[g - 2].astype(bf16)

    @pl.when(step == HEADS // GROUP - 1)
    def _():
        for g in range(2):
            for m in range(7):
                turned = pltpu.roll(rest[g], (HEAD_DIM - 16 * m) % PAD, 1).astype(bf16)
                o_ref[pl.ds((7 * g + m) * HEAD_DIM, HEAD_DIM), HEAD_DIM:] = turned[:, HEAD_DIM:]
        o_ref[pl.ds(FULL * HEAD_DIM, 32), :] = norm_ref[...].astype(bf16)


def states(k_t, v_t):
    tokens = k_t.shape[1]
    spec = pl.BlockSpec((GROUP * HEAD_DIM, tokens), lambda i: (i, 0))
    return pl.pallas_call(
        state_kernel,
        grid=(HEADS // GROUP,),
        in_specs=[spec, spec],
        out_specs=pl.BlockSpec((2048, PAD), lambda i: (0, 0)),
        out_shape=jax.ShapeDtypeStruct((2048, PAD), bf16),
        scratch_shapes=[pltpu.VMEM((32, PAD), f32)],
        compiler_params=pltpu.CompilerParams(vmem_limit_bytes=SMALL),
        name="states",
        cost_estimate=pl.CostEstimate(
            flops=2 * HEADS * PAD * PAD * tokens, bytes_accessed=4 * D * tokens, transcendentals=0
        ),
    )(k_t, v_t)


def in_tile_kernel(z_ref, r_ref, o_ref):
    z = z_ref[0]
    inclusive = None
    for x in range(NX):
        own = r_ref[x * 8].astype(f32)
        for s in range(1, 8):
            own = own + r_ref[x * 8 + s].astype(f32)
        exclusive = jnp.zeros_like(own) if inclusive is None else inclusive
        inclusive = exclusive + own
        later, earlier = inclusive.astype(bf16), exclusive.astype(bf16)
        for t in range(NZ):
            keep = (jnp.full(later.shape, t, jnp.int32) >= z).astype(f32)
            o_ref[t, x] = jnp.where(keep > 0, later.astype(f32), earlier.astype(f32)).astype(bf16)


def small_call(kernel, shape, scalars, arrays, scratch=()):
    return pl.pallas_call(
        kernel,
        in_specs=[pl.BlockSpec(memory_space=pltpu.SMEM)] * len(scalars)
        + [pl.BlockSpec(memory_space=pltpu.VMEM)] * len(arrays),
        out_specs=jax.tree.map(lambda _: pl.BlockSpec(memory_space=pltpu.VMEM), shape),
        out_shape=shape,
        scratch_shapes=list(scratch),
        compiler_params=pltpu.CompilerParams(vmem_limit_bytes=SMALL),
        cost_estimate=pl.CostEstimate(flops=1000000, bytes_accessed=2000000, transcendentals=0),
    )(*scalars, *arrays)


def prefix_kernel(r_ref, o_ref):
    for x in range(NX):
        total = r_ref[0, x].astype(f32)
        for t in range(1, NZ):
            total = total + r_ref[t, x].astype(f32)
        total = total.astype(bf16)
        for s in range(8):
            o_ref[x, s] = total


def slab_kernel(at_ref, w_ref, o_ref, r_ref):
    slab, core = at_ref[0], at_ref[1]
    main = w_ref[:, pl.ds(pl.multiple_of(slab * 256, 256), 256)]
    first = w_ref[:, 2048:2176].astype(f32)
    last = w_ref[:, 2176:2240].astype(f32)
    last = jnp.concatenate([last, jnp.zeros_like(last)], axis=1)
    pick = jnp.full(first.shape, core, jnp.int32) == 0
    r_ref[...] = jnp.where(pick, first, last).astype(bf16)
    for t in range(NZ):
        o_ref[t] = main


def compact_kernel(w_ref, r0, r1, r2, r3, x_ref, y_ref, r_ref, rows_ref):
    rows = w_ref.shape[1]
    for t in range(NZ):
        rows_ref[pl.ds(t * rows, rows), :] = w_ref[t].astype(f32)
    slab = rows_ref[...].astype(bf16)
    x_ref[...] = slab[:, :128]
    y_ref[...] = slab[:, 128:]
    for k, piece in enumerate((r0, r1, r2, r3)):
        r_ref[k] = piece[...]


def edge_kernel(z_ref, *refs):
    pieces, (o_ref, rows_ref) = refs[:NZ], refs[NZ:]
    rows = pieces[0].shape[1]
    z = z_ref[0]
    for own in range(NZ):

        @pl.when(z == own)
        def _():
            for t in range(NZ):
                for k in range(NX):
                    at = k * ROWS_X + (own - t) % NZ * rows
                    rows_ref[pl.ds(at, rows), :] = pieces[t][k].astype(f32)

    for k in range(NX):
        o_ref[k] = rows_ref[pl.ds(k * ROWS_X, ROWS_X), :].astype(bf16)


def stack_kernel(*refs):
    by_x, by_y, (main_x, main_y, every) = refs[:4], refs[4:8], refs[8:]
    for k in range(4):
        main_x[k] = by_x[k][...]
        main_y[k] = by_y[k][...]
        every[k] = by_x[k][...]
        every[4 + k] = by_y[k][...]


def project_kernel(at_ref, q_ref, p_ref, g_ref, *refs):
    parts, (o_ref, w_ref, mixed_ref, normed_ref, sem) = refs[:16], refs[16:]
    x, y, core = at_ref[0], at_ref[1], at_ref[2]
    copies = []

    def fetch(source, block, column):
        rows = pl.ds(pl.multiple_of(block * ROWS_X, 16), ROWS_X)
        target = w_ref.at[rows, pl.ds(pl.multiple_of(column, 128), 128)]
        copies.append(pltpu.make_async_copy(source, target, sem.at[len(copies)]))
        copies[-1].start()

    for side in range(NC):
        which = core if side == 0 else 1 - core
        every, *rest = parts[8 * side : 8 * side + 8]
        by_y, by_x = (every.at[pl.ds(0, 4)], *rest[:3]), (every.at[pl.ds(4, 4)], *rest[3:6])
        edges = rest[6]
        for k in range(4):
            block = lax.rem(x - k + NX, NX)
            column = which * 1024 + lax.rem(y - k + NY, NY) * 256
            fetch(edges.at[k], block, 2048 + which * 128)
            for n in range(4):
                turn = lax.rem(y - n + NY, NY)
                fetch(by_y[n].at[k], block, which * 1024 + turn * 256)
                turn = lax.rem(x - n + NX, NX)
                fetch(by_x[n].at[k], turn, column + 128)
    tokens = q_ref.shape[1]
    squares = jnp.zeros((1, tokens), f32)
    lane = lax.broadcasted_iota(jnp.int32, (HEAD_DIM, PAD), 1) // 16
    for h in range(HEADS):
        rows = pl.ds(h * HEAD_DIM, HEAD_DIM)
        fq = jnp.maximum(q_ref[rows, :], 0)
        if h < FULL:
            state = p_ref[rows, :]
        else:
            state = jnp.zeros((HEAD_DIM, PAD), f32)
            for m in range(7):
                piece = p_ref[pl.ds((7 * (h - FULL) + m) * HEAD_DIM, HEAD_DIM), :].astype(f32)
                state = jnp.where(lane == m, pltpu.roll(piece, (16 + 16 * m) % PAD, 1), state)
            state = state.astype(bf16)
        norms = p_ref[pl.ds(FULL * HEAD_DIM + h // 16 * 16, 16), :]
        prefix = jnp.concatenate([state, norms], axis=0)[:, :HEAD_DIM]
        sums = jnp.dot(prefix, fq, preferred_element_type=f32)
        norm = sums[HEAD_DIM + h % 16 : HEAD_DIM + h % 16 + 1]
        mixed = sums[:HEAD_DIM] * (1.0 / (norm + 1.0))
        squares = squares + jnp.sum(mixed * mixed, axis=0, keepdims=True)
        mixed_ref[rows, :] = mixed
    scale = lax.rsqrt(squares * (1.0 / D) + 1e-06)
    for i in range(0, D, 256):
        width = min(256, D - i)
        rows = pl.ds(i, width)
        normed = (mixed_ref[rows, :] * scale * g_ref[rows, :]).astype(bf16)
        normed_ref[:, pl.ds(i, width)] = normed.T
    for copy in copies:
        copy.wait()
    for j in range(0, D, 256):
        width = min(256, D - j)
        total = jnp.dot(normed_ref[...], w_ref[:, pl.ds(j, 256)], preferred_element_type=f32)
        o_ref[pl.ds(j, width), :] = total.astype(bf16).T[:width]


def project(at, q_t, prefix, gain, parts):
    tokens = q_t.shape[1]
    vmem = pl.BlockSpec(memory_space=pltpu.VMEM)
    anyw = pl.BlockSpec(memory_space=pl.ANY)
    return pl.pallas_call(
        project_kernel,
        in_specs=[pl.BlockSpec(memory_space=pltpu.SMEM), vmem, vmem, vmem] + [anyw] * 16,
        out_specs=vmem,
        out_shape=jax.ShapeDtypeStruct((D, tokens), bf16),
        scratch_shapes=[
            pltpu.VMEM((D, COLS), bf16),
            pltpu.VMEM((D, tokens), f32),
            pltpu.VMEM((tokens, D), bf16),
            pltpu.SemaphoreType.DMA((72,)),
        ],
        compiler_params=pltpu.CompilerParams(vmem_limit_bytes=BIG),
        name="project",
        cost_estimate=pl.CostEstimate(
            flops=2 * D * D * tokens, bytes_accessed=2 * D * COLS + 4 * D * tokens, transcendentals=0
        ),
    )(at, q_t, prefix, gain, *parts)


def swap(value, axes):
    return lax.all_to_all(value, axes, split_axis=0, concat_axis=0, tiled=True)


def moved(value, axis, step):
    n = lax.axis_size(axis)
    return lax.ppermute(value, axis, [(i, (i + step) % n) for i in range(n)])


def shifted(value, axis):
    return [moved(value, axis, k) for k in range(1, lax.axis_size(axis))]


def after(value, *others):
    return lax.optimization_barrier((value, *others))[0]


def step(queries, keys, values, gain, out_weight):
    q_t, k_t, v_t = (jnp.swapaxes(a[0], 0, 1) for a in (queries, keys, values))
    z, y, core = lax.axis_index("z"), lax.axis_index("y"), lax.axis_index("core")
    rows = out_weight.shape[0]
    at = jnp.stack([core * NY + y, core]).astype(jnp.int32)
    zs = z.astype(jnp.int32).reshape(1)
    rows = out_weight.shape[0]
    slab, rest = small_call(
        slab_kernel,
        (jax.ShapeDtypeStruct((NZ, rows, 256), bf16), jax.ShapeDtypeStruct((rows, 128), bf16)),
        (at,),
        (out_weight,),
    )
    w_z = swap(slab, "z")
    rest = [rest, *shifted(rest, "x")]
    k_t, v_t = (pltpu.with_memory_space_constraint(a, pltpu.HBM) for a in (k_t, v_t))
    st = after(states(k_t, v_t), w_z)
    r1 = swap(st.reshape(32, PART, PAD), PIECES)
    x0, y0, r0 = small_call(
        compact_kernel,
        (jax.ShapeDtypeStruct((ROWS_X, 128), bf16),) * 2
        + (jax.ShapeDtypeStruct((NX, rows, 128), bf16),),
        (),
        (w_z, *rest),
        (pltpu.VMEM((NZ * rows, 256), f32),),
    )
    by_x = [x0, *shifted(x0, "x")]
    by_y = [y0, *shifted(y0, "y")]
    r2 = small_call(in_tile_kernel, jax.ShapeDtypeStruct((NZ, NX, PART, PAD), bf16), (zs,), (r1,))
    r2s = swap(r2, "z")
    four = jax.ShapeDtypeStruct((4, ROWS_X, 128), bf16)
    main_x, main_y, every = small_call(
        stack_kernel, (four, four, jax.ShapeDtypeStruct((8, ROWS_X, 128), bf16)), (), (*by_x, *by_y)
    )
    parts = [every, *shifted(main_x, "y"), *shifted(main_y, "x")]
    edge = small_call(
        edge_kernel, four, (zs,), (r0, *shifted(r0, "z")), (pltpu.VMEM((D, 128), f32),)
    )
    parts.append(edge)
    r3 = small_call(prefix_kernel, jax.ShapeDtypeStruct((NX, 8, PART, PAD), bf16), (), (r2s,))
    prefix = swap(r3.reshape(32, PART, PAD), PIECES).reshape(2048, PAD)
    parts += [moved(part, "core", 1) for part in parts]
    at = jnp.stack([lax.axis_index("x"), y, core]).astype(jnp.int32)
    out = project(at, q_t, prefix, gain.reshape(D, 1), parts)
    return jnp.swapaxes(out, 0, 1)[None]


def solution(mesh):
    finer = Mesh(mesh.devices.reshape(NX, NZ, NY, NC), ("x", "z", "y", "core"))
    tokens = P(TM, ("y", "core"), None)
    return jax.shard_map(
        step,
        mesh=finer,
        in_specs=(tokens, tokens, tokens, P(), P(TM, None)),
        out_specs=tokens,
        check_vma=False,
    )
```

```python
import functools

import jax
import jax.numpy as jnp
from jax import lax
from jax.experimental import pallas as pl
from jax.experimental.pallas import tpu as pltpu
from jax.sharding import Mesh
from jax.sharding import PartitionSpec as P

HEADS = 20
HEAD_DIM = 112
D = HEADS * HEAD_DIM
PAD = 128
GROUP = 4
FULL = 18
PART = 64
bf16 = jnp.bfloat16
f32 = jnp.float32
TM = ("x", "z")
PIECES = ("x", "y", "core")
NX, NZ, NY, NC = 4, 8, 4, 2
ROWS_X = D // NX
COLS = 2304
BIG = 16 * 1024 * 1024
SMALL = 12 * 1024 * 1024


def state_kernel(k_ref, v_ref, o_ref, norm_ref):
    tokens = k_ref.shape[1]
    step = pl.program_id(0)
    ones = jnp.ones((PAD - HEAD_DIM, tokens), bf16)

    def state_of(g):
        rows = pl.ds(g * HEAD_DIM, HEAD_DIM)
        fk = jnp.maximum(k_ref[rows, :], 0)
        vals = jnp.concatenate([v_ref[rows, :], ones], axis=0)
        state = lax.dot_general(vals, fk, (((1,), (1,)), ((), ())), preferred_element_type=f32)
        state = jnp.concatenate([state, jnp.zeros((PAD, PAD - HEAD_DIM), f32)], axis=1)
        norm_ref[pl.ds(step * GROUP + g, 1), :] = state[HEAD_DIM : HEAD_DIM + 1]
        return state[:HEAD_DIM]

    @pl.when(step == 0)
    def _():
        norm_ref[...] = jnp.zeros_like(norm_ref)

    for g in range(2):
        at = pl.multiple_of((step * GROUP + g) * HEAD_DIM, 16)
        o_ref[pl.ds(at, HEAD_DIM), :] = state_of(g).astype(bf16)
    rest = [state_of(g) for g in range(2, GROUP)]

    @pl.when(step < HEADS // GROUP - 1)
    def _():
        for g in range(2, GROUP):
            at = pl.multiple_of((step * GROUP + g) * HEAD_DIM, 16)
            o_ref[pl.ds(at, HEAD_DIM), :] = rest[g - 2].astype(bf16)

    @pl.when(step == HEADS // GROUP - 1)
    def _():
        for g in range(2):
            for m in range(7):
                turned = pltpu.roll(rest[g], (HEAD_DIM - 16 * m) % PAD, 1).astype(bf16)
                o_ref[pl.ds((7 * g + m) * HEAD_DIM, HEAD_DIM), HEAD_DIM:] = turned[:, HEAD_DIM:]
        o_ref[pl.ds(FULL * HEAD_DIM, 32), :] = norm_ref[...].astype(bf16)


def states(k_t, v_t):
    tokens = k_t.shape[1]
    spec = pl.BlockSpec((GROUP * HEAD_DIM, tokens), lambda i: (i, 0))
    return pl.pallas_call(
        state_kernel,
        grid=(HEADS // GROUP,),
        in_specs=[spec, spec],
        out_specs=pl.BlockSpec((2048, PAD), lambda i: (0, 0)),
        out_shape=jax.ShapeDtypeStruct((2048, PAD), bf16),
        scratch_shapes=[pltpu.VMEM((32, PAD), f32)],
        compiler_params=pltpu.CompilerParams(vmem_limit_bytes=SMALL),
        name="states",
        cost_estimate=pl.CostEstimate(
            flops=2 * HEADS * PAD * PAD * tokens, bytes_accessed=4 * D * tokens, transcendentals=0
        ),
    )(k_t, v_t)


def in_tile_kernel(z_ref, r_ref, o_ref):
    z = z_ref[0]
    inclusive = None
    for x in range(NX):
        own = r_ref[x * 8].astype(f32)
        for s in range(1, 8):
            own = own + r_ref[x * 8 + s].astype(f32)
        exclusive = jnp.zeros_like(own) if inclusive is None else inclusive
        inclusive = exclusive + own
        later, earlier = inclusive.astype(bf16), exclusive.astype(bf16)
        for t in range(NZ):
            keep = (jnp.full(later.shape, t, jnp.int32) >= z).astype(f32)
            o_ref[t, x] = jnp.where(keep > 0, later.astype(f32), earlier.astype(f32)).astype(bf16)


def small_call(kernel, shape, scalars, arrays, scratch=()):
    return pl.pallas_call(
        kernel,
        in_specs=[pl.BlockSpec(memory_space=pltpu.SMEM)] * len(scalars)
        + [pl.BlockSpec(memory_space=pltpu.VMEM)] * len(arrays),
        out_specs=jax.tree.map(lambda _: pl.BlockSpec(memory_space=pltpu.VMEM), shape),
        out_shape=shape,
        scratch_shapes=list(scratch),
        compiler_params=pltpu.CompilerParams(vmem_limit_bytes=SMALL),
        cost_estimate=pl.CostEstimate(flops=1000000, bytes_accessed=2000000, transcendentals=0),
    )(*scalars, *arrays)


def prefix_kernel(r_ref, o_ref):
    for x in range(NX):
        total = r_ref[0, x].astype(f32)
        for t in range(1, NZ):
            total = total + r_ref[t, x].astype(f32)
        total = total.astype(bf16)
        for s in range(8):
            o_ref[x, s] = total


def slab_kernel(at_ref, w_ref, o_ref, r_ref):
    slab, core = at_ref[0], at_ref[1]
    main = w_ref[:, pl.ds(pl.multiple_of(slab * 256, 256), 256)]
    first = w_ref[:, 2048:2176].astype(f32)
    last = w_ref[:, 2176:2240].astype(f32)
    last = jnp.concatenate([last, jnp.zeros_like(last)], axis=1)
    pick = jnp.full(first.shape, core, jnp.int32) == 0
    r_ref[...] = jnp.where(pick, first, last).astype(bf16)
    for t in range(NZ):
        o_ref[t] = main


def compact_kernel(w_ref, r0, r1, r2, r3, x_ref, y_ref, r_ref, rows_ref):
    rows = w_ref.shape[1]
    for t in range(NZ):
        rows_ref[pl.ds(t * rows, rows), :] = w_ref[t].astype(f32)
    slab = rows_ref[...].astype(bf16)
    x_ref[...] = slab[:, :128]
    y_ref[...] = slab[:, 128:]
    for k, piece in enumerate((r0, r1, r2, r3)):
        r_ref[k] = piece[...]


def edge_kernel(z_ref, *refs):
    pieces, (o_ref, rows_ref) = refs[:NZ], refs[NZ:]
    rows = pieces[0].shape[1]
    z = z_ref[0]
    for own in range(NZ):

        @pl.when(z == own)
        def _():
            for t in range(NZ):
                for k in range(NX):
                    at = k * ROWS_X + (own - t) % NZ * rows
                    rows_ref[pl.ds(at, rows), :] = pieces[t][k].astype(f32)

    for k in range(NX):
        o_ref[k] = rows_ref[pl.ds(k * ROWS_X, ROWS_X), :].astype(bf16)


def stack_kernel(*refs):
    by_x, by_y, (main_x, main_y, every) = refs[:4], refs[4:8], refs[8:]
    for k in range(4):
        main_x[k] = by_x[k][...]
        main_y[k] = by_y[k][...]
        every[k] = by_x[k][...]
        every[4 + k] = by_y[k][...]


def mix_kernel(q_ref, p_ref, g_ref, o_ref, mixed_ref):
    tokens = q_ref.shape[1]
    squares = jnp.zeros((1, tokens), f32)
    lane = lax.broadcasted_iota(jnp.int32, (HEAD_DIM, PAD), 1) // 16
    for h in range(HEADS):
        rows = pl.ds(h * HEAD_DIM, HEAD_DIM)
        fq = jnp.maximum(q_ref[rows, :], 0)
        if h < FULL:
            state = p_ref[rows, :]
        else:
            state = jnp.zeros((HEAD_DIM, PAD), f32)
            for m in range(7):
                piece = p_ref[pl.ds((7 * (h - FULL) + m) * HEAD_DIM, HEAD_DIM), :].astype(f32)
                state = jnp.where(lane == m, pltpu.roll(piece, (16 + 16 * m) % PAD, 1), state)
            state = state.astype(bf16)
        norms = p_ref[pl.ds(FULL * HEAD_DIM + h // 16 * 16, 16), :]
        prefix = jnp.concatenate([state, norms], axis=0)[:, :HEAD_DIM]
        sums = jnp.dot(prefix, fq, preferred_element_type=f32)
        norm = sums[HEAD_DIM + h % 16 : HEAD_DIM + h % 16 + 1]
        mixed = sums[:HEAD_DIM] * (1.0 / (norm + 1.0))
        squares = squares + jnp.sum(mixed * mixed, axis=0, keepdims=True)
        mixed_ref[rows, :] = mixed
    scale = lax.rsqrt(squares * (1.0 / D) + 1e-06)
    for i in range(0, D, 256):
        width = min(256, D - i)
        rows = pl.ds(i, width)
        normed = (mixed_ref[rows, :] * scale * g_ref[rows, :]).astype(bf16)
        o_ref[:, pl.ds(i, width)] = normed.T


def mix(q_t, prefix, gain):
    tokens = q_t.shape[1]
    vmem = pl.BlockSpec(memory_space=pltpu.VMEM)
    return pl.pallas_call(
        mix_kernel,
        in_specs=[vmem] * 3,
        out_specs=vmem,
        out_shape=jax.ShapeDtypeStruct((tokens, D), bf16),
        scratch_shapes=[pltpu.VMEM((D, tokens), f32)],
        compiler_params=pltpu.CompilerParams(vmem_limit_bytes=BIG),
        name="mix",
        cost_estimate=pl.CostEstimate(
            flops=2 * D * PAD * tokens, bytes_accessed=4 * D * tokens, transcendentals=0
        ),
    )(q_t, prefix, gain)


def project_kernel(count, at_ref, n_ref, every, y1, y2, y3, x1, x2, x3, *refs):
    edges = refs[: count - 4]
    o_ref, w_ref, out_ref, sem, out_sem = refs[-5:]
    x, y, which = at_ref[0], at_ref[1], at_ref[2]
    by_y, by_x = (every.at[pl.ds(0, 4)], y1, y2, y3), (every.at[pl.ds(4, 4)], x1, x2, x3)
    copies = []

    def fetch(source, block, column):
        rows = pl.ds(pl.multiple_of(block * ROWS_X, 16), ROWS_X)
        target = w_ref.at[rows, pl.ds(pl.multiple_of(column, 128), 128)]
        copies.append(pltpu.make_async_copy(source, target, sem.at[len(copies)]))
        copies[-1].start()

    for k in range(4):
        block = lax.rem(x - k + NX, NX)
        for n in range(4):
            fetch(by_y[n].at[k], block, n * 256)
            fetch(by_x[k].at[n], block, n * 256 + 128)
        for side, edge in zip((which, 1 - which), edges):
            fetch(edge.at[k], block, 1024 + side * 128)
    for copy in copies:
        copy.wait()
    for n in range(4 + len(edges) // 2):
        total = jnp.dot(n_ref[...], w_ref[:, pl.ds(n * 256, 256)], preferred_element_type=f32)
        out_ref[pl.ds(n * 256, 256), :] = total.astype(bf16).T
    stores = []
    for n in range(4):
        at = pl.multiple_of(which * 1024 + lax.rem(y - n + NY, NY) * 256, 256)
        stores.append((n * 256, at, 256))
    if edges:
        stores.append((1024, 2048, D - 2048))
    stores = [
        pltpu.make_async_copy(
            out_ref.at[pl.ds(start, size), :], o_ref.at[pl.ds(at, size), :], out_sem.at[i]
        )
        for i, (start, at, size) in enumerate(stores)
    ]
    for store in stores:
        store.start()
    for store in stores:
        store.wait()


def project(at, normed, parts, edges=(), out=None):
    tokens = normed.shape[0]
    vmem = pl.BlockSpec(memory_space=pltpu.VMEM)
    anyw = pl.BlockSpec(memory_space=pl.ANY)
    extra = [*edges] if out is None else [*edges, out]
    return pl.pallas_call(
        functools.partial(project_kernel, 4 + len(edges)),
        in_specs=[pl.BlockSpec(memory_space=pltpu.SMEM), vmem] + [anyw] * (7 + len(extra)),
        out_specs=anyw,
        out_shape=jax.ShapeDtypeStruct((D, tokens), bf16),
        input_output_aliases={} if out is None else {8 + len(extra): 0},
        scratch_shapes=[
            pltpu.VMEM((D, 1280), bf16),
            pltpu.VMEM((1280, tokens), bf16),
            pltpu.SemaphoreType.DMA((40,)),
            pltpu.SemaphoreType.DMA((5,)),
        ],
        compiler_params=pltpu.CompilerParams(vmem_limit_bytes=16 * 1024 * 1024),
        cost_estimate=pl.CostEstimate(
            flops=D * D * tokens, bytes_accessed=D * COLS + 3 * D * tokens, transcendentals=0
        ),
    )(at, normed, *parts, *extra)


def swap(value, axes):
    return lax.all_to_all(value, axes, split_axis=0, concat_axis=0, tiled=True)


def moved(value, axis, step):
    n = lax.axis_size(axis)
    return lax.ppermute(value, axis, [(i, (i + step) % n) for i in range(n)])


def shifted(value, axis):
    return [moved(value, axis, k) for k in range(1, lax.axis_size(axis))]


def after(value, *others):
    return lax.optimization_barrier((value, *others))[0]


def step(queries, keys, values, gain, out_weight):
    q_t, k_t, v_t = (jnp.swapaxes(a[0], 0, 1) for a in (queries, keys, values))
    z, y, core = lax.axis_index("z"), lax.axis_index("y"), lax.axis_index("core")
    rows = out_weight.shape[0]
    at = jnp.stack([core * NY + y, core]).astype(jnp.int32)
    zs = z.astype(jnp.int32).reshape(1)
    rows = out_weight.shape[0]
    slab, rest = small_call(
        slab_kernel,
        (jax.ShapeDtypeStruct((NZ, rows, 256), bf16), jax.ShapeDtypeStruct((rows, 128), bf16)),
        (at,),
        (out_weight,),
    )
    w_z = swap(slab, "z")
    rest = [rest, *shifted(rest, "x")]
    k_t, v_t = (pltpu.with_memory_space_constraint(a, pltpu.HBM) for a in (k_t, v_t))
    st = after(states(k_t, v_t), w_z)
    r1 = swap(st.reshape(32, PART, PAD), PIECES)
    x0, y0, r0 = small_call(
        compact_kernel,
        (jax.ShapeDtypeStruct((ROWS_X, 128), bf16),) * 2
        + (jax.ShapeDtypeStruct((NX, rows, 128), bf16),),
        (),
        (w_z, *rest),
        (pltpu.VMEM((NZ * rows, 256), f32),),
    )
    by_x = [x0, *shifted(x0, "x")]
    by_y = [y0, *shifted(y0, "y")]
    r2 = small_call(in_tile_kernel, jax.ShapeDtypeStruct((NZ, NX, PART, PAD), bf16), (zs,), (r1,))
    r2s = swap(r2, "z")
    four = jax.ShapeDtypeStruct((4, ROWS_X, 128), bf16)
    main_x, main_y, every = small_call(
        stack_kernel, (four, four, jax.ShapeDtypeStruct((8, ROWS_X, 128), bf16)), (), (*by_x, *by_y)
    )
    parts = [every, *shifted(main_x, "y"), *shifted(main_y, "x")]
    edge = small_call(
        edge_kernel, four, (zs,), (r0, *shifted(r0, "z")), (pltpu.VMEM((D, 128), f32),)
    )
    parts.append(edge)
    r3 = small_call(prefix_kernel, jax.ShapeDtypeStruct((NX, 8, PART, PAD), bf16), (), (r2s,))
    prefix = swap(r3.reshape(32, PART, PAD), PIECES).reshape(2048, PAD)
    *other, edge2 = [moved(part, "core", 1) for part in parts]
    *parts, edge = parts
    normed = mix(q_t, prefix, gain.reshape(D, 1))
    place = [lax.axis_index("x"), y]
    at = [jnp.stack([*place, side]).astype(jnp.int32) for side in (core, 1 - core)]
    out = project(at[0], normed, parts)
    out = project(at[1], normed, other, (edge2, edge), out)
    return jnp.swapaxes(out, 0, 1)[None]


def solution(mesh):
    finer = Mesh(mesh.devices.reshape(NX, NZ, NY, NC), ("x", "z", "y", "core"))
    tokens = P(TM, ("y", "core"), None)
    return jax.shard_map(
        step,
        mesh=finer,
        in_specs=(tokens, tokens, tokens, P(), P(TM, None)),
        out_specs=tokens,
        check_vma=False,
    )
```
